32 devices in a mesh: groups: 2 (over y), expert: 4 (over z), replica: 4 (over x, core).
Axes of the slice: x: 2, y: 2, z: 4, core: 2. Of those that a mesh axis runs over, the one named last changes fastest.
Arguments:
- tokens: bfloat16 [4096, 1024], P(('groups', 'expert', 'replica')), parts along dimension 0, may hold values from -6 to 6
- expert_ids: int32 [4096, 6], P(('groups', 'expert', 'replica')), parts along dimension 0, may hold values from 0 to 15, all different within a row; in each aligned block of 128 rows (0 to 127, 128 to 255, ...) at most 64 rows name the same one
- gate_probs: bfloat16 [4096, 6], P(('groups', 'expert', 'replica')), parts along dimension 0, may hold values from 0.099609375 to 0.59765625
- cotangent: bfloat16 [4096, 1024], P(('groups', 'expert', 'replica')), parts along dimension 0, may hold values from -1.5 to 1.5
- gate_up: bfloat16 [1024, 16, 1536], P(None, 'expert'), may hold values from -0.1875 to 0.1875
- down_weights: bfloat16 [768, 16, 1024], P(None, 'expert'), may hold values from -0.21875 to 0.21875
Outputs:
- combined: bfloat16 [4096, 1024], P(('groups', 'expert', 'replica')), parts along dimension 0
- token_gradient: bfloat16 [4096, 1024], P(('groups', 'expert', 'replica')), parts along dimension 0
- prob_gradient: float32 [4096, 6], P(('groups', 'expert', 'replica')), parts along dimension 0
- gate_up_gradient: float32 [2048, 16, 1536], P(('groups', 'replica'), 'expert'), parts along dimension 0
- down_gradient: float32 [1536, 16, 1024], P(('groups', 'replica'), 'expert'), parts along dimension 0
The draws below stay inside these ranges and needn't reach their ends.
There are 2 independent parts, one for each index of `groups`. The reference program is written for one: setup_inputs(seed, part) draws one part's arguments, and reference() takes and returns one part's arrays. A program takes and returns all parts, laid end to end along the dimension named above; an argument that names none is the same for every part. Nothing has to cross between parts.
Inputs may be any that keep to these rules, and one draw needn't show every extreme that they name: `expert_ids`: each row names 6 different experts. Within the rows of one device (aligned blocks of 128 rows) no expert is named by more than 64 rows, and in some block one expert is named by exactly 64 rows.
All inputs are finite; a program needn't handle non-finite values.
Results may differ from the reference program's by a relative error of at most 0.0064.
Values may be sent and summed in bfloat16 or wider, within the bound.
A program may use at most 128 MiB of HBM per device.

```python
import math
import jax
import jax.numpy as jnp
import numpy as np
from jax import lax

D = 1024
FF = 768
TOP = 6
EXPERTS = 16
TOK_DEV = 128
CAP = 64
TOKENS = 2048
N_EXPERT = 4
N_REPLICA = 4


def level_of(key, shape, split, low, top_value):
    loudness = 1.0
    for dim, shards_of in split:
        draws = jax.random.uniform(jax.random.fold_in(jax.random.fold_in(key, 6), dim), (shards_of,), jnp.float32, low / len(split), top_value / len(split))
        loudness = loudness * jnp.repeat(jnp.exp(draws), shape[dim] // shards_of).reshape((-1,) + (1,) * (len(shape) - 1 - dim))
    return loudness


def assign_block(stream_key, own, number, rows, count, top, reach, slope):
    order = jax.random.permutation(stream_key, count)
    heavy_load, common = portions_of(count, rows * top, reach, slope, True), portions_of(count, rows * top, reach, slope, False)
    places = jnp.arange(count)

    def named(tallies, offset_by):
        used = int((tallies > 0).sum())
        fixed = max(1, used // 4)
        passed = fixed + (places - fixed + offset_by * (used - fixed)) % max(1, count - fixed)
        return jnp.zeros((count,), jnp.int32).at[order[jnp.where(places < fixed, places, passed)]].set(jnp.asarray(tallies, jnp.int32))

    tallies = jnp.where(number % 4 == 0, named(heavy_load, number // 4), named(common, number - number // 4 - 1))
    mixed = jax.random.permutation(jax.random.fold_in(own, 3), count)
    source_of, sink = mixed[0:count // 2 * 2:2], mixed[1:count // 2 * 2:2]
    margin = jnp.minimum(tallies[source_of] - 1, reach - tallies[sink]) // 2
    margin = jnp.where((source_of == order[0]) | (sink == order[0]) | (tallies[sink] == 0), 0, jnp.maximum(margin, 0))
    passed = jax.random.randint(jax.random.fold_in(own, 4), (count // 2,), 0, 1 << 20) % (margin + 1)
    tallies = tallies.at[source_of].add(-passed).at[sink].add(passed)
    members = jnp.searchsorted(jnp.cumsum(tallies), jnp.arange(rows * top), side="right").astype(jnp.int32)
    grid = members.reshape(top, rows).T
    grid = grid[jax.random.permutation(jax.random.fold_in(own, 1), rows)]
    offset_by = jax.random.randint(jax.random.fold_in(own, 2), (rows, 1), 0, top)
    return jnp.take_along_axis(grid, (jnp.arange(top)[None, :] + offset_by) % top, axis=1)


def portions_of(number_of, total, limit, slope, full):
    loads = [(1 << 20) // math.isqrt(grade ** slope) + 1 for grade in range(1, number_of + 1)]
    largest = limit if full else min(limit, max(-(-total // number_of), total * loads[0] // sum(loads)))
    least = 1 if total - largest >= number_of - 1 else 0
    given, rest = [largest] + [least] * (number_of - 1), total - largest - least * (number_of - 1)
    while rest > 0:
        candidates = [i for i in range(1, number_of) if given[i] < largest] or [i for i in range(1, number_of) if given[i] < limit]
        pool, budget = sum([loads[i] for i in candidates]), rest
        for i in candidates:
            addition = min(limit - given[i], max(1, budget * loads[i] // pool), rest)
            given[i] = given[i] + addition
            rest = rest - addition
    return np.array(given)


def gaussian(stream_key, shape, spread, bound, pieces=(), kind=jnp.bfloat16):
    drawn = jax.random.normal(stream_key, shape, jnp.float32) * spread
    if len(pieces) > 0:
        drawn = level_of(stream_key, shape, pieces, -0.22, 0.18) * drawn
    return jnp.clip(drawn, min=-bound, max=bound).astype(kind)


def setup_inputs(seed: int = 0, part: int = 0) -> dict:
    seeds = jax.random.split(jax.random.key(seed), 7)
    part_splits = jax.random.split(jax.random.fold_in(seeds[6], part), 7)
    tokens = gaussian(part_splits[0], (TOKENS, D), 1.0, 6.0, ((0, 16),))
    expert_ids_keys = jax.random.split(jax.random.fold_in(part_splits[1], 1), TOKENS // TOK_DEV)
    expert_ids_turns = jax.random.permutation(jax.random.fold_in(part_splits[1], 3), TOKENS // TOK_DEV)
    expert_ids = jax.vmap(lambda own, number: assign_block(jax.random.fold_in(part_splits[1], 2), own, number, TOK_DEV, EXPERTS, TOP, CAP, 1))(expert_ids_keys, expert_ids_turns).reshape((TOKENS, TOP))
    gate_probs = jnp.clip(0.099609375 + 0.49804688 * jax.random.uniform(part_splits[2], (TOKENS, TOP), jnp.float32) ** level_of(part_splits[2], (TOKENS, TOP), ((0, 16),), -0.2, 0.2), 0.099609375, 0.59765625).astype(jnp.bfloat16)
    cotangent = gaussian(part_splits[3], (TOKENS, D), 0.25, 1.5, ((0, 16),))
    gate_up = gaussian(seeds[4], (D, EXPERTS, 2 * FF), D ** -0.5, 0.1875, ((1, 4),))
    down_weights = gaussian(seeds[5], (FF, EXPERTS, D), FF ** -0.5, 0.21875, ((1, 4),))
    return {"tokens": tokens, "expert_ids": expert_ids, "gate_probs": gate_probs, "cotangent": cotangent, "gate_up": gate_up, "down_weights": down_weights}


def slot_table(expert_ids, experts, capacity):
    flat_ids = expert_ids.reshape(-1)
    assigned = flat_ids.shape[0]
    onehot = (flat_ids[:, None] == jnp.arange(experts, dtype=jnp.int32)[None, :]).astype(jnp.int32)
    before = jnp.cumsum(onehot, axis=0) - onehot
    slot_index = jnp.sum(before * onehot, axis=1).astype(jnp.int32)
    position = (flat_ids * capacity + slot_index).astype(jnp.int32)
    slot_owner = jnp.full((experts * capacity,), assigned, jnp.int32).at[position].set(jnp.arange(assigned, dtype=jnp.int32))
    return position, slot_owner


def regroup(values):
    return values.reshape(N_EXPERT, EXPERTS, CAP, -1).swapaxes(0, 1).reshape(EXPERTS, N_EXPERT * CAP, -1)


def ungroup(values):
    return values.reshape(EXPERTS, N_EXPERT, CAP, -1).swapaxes(0, 1).reshape(N_EXPERT, EXPERTS * CAP, -1)


def split_rows(values):
    return values.reshape((N_EXPERT, N_REPLICA, TOK_DEV) + values.shape[1:]).swapaxes(0, 1)


def join_rows(values):
    return values.swapaxes(0, 1).reshape((TOKENS,) + values.shape[3:])


def reference(tokens, expert_ids, gate_probs, cotangent, gate_up, down_weights):
    gate_float = gate_up.astype(jnp.float32)
    down_float = down_weights.astype(jnp.float32)

    def one_row(carry, row_data):
        row_tokens, row_ids, row_probs, row_cot = row_data
        position, slot_owner = jax.vmap(lambda choose: slot_table(choose, EXPERTS, CAP))(row_ids)
        zero_rows = jnp.zeros((N_EXPERT, 1, D), jnp.bfloat16)
        padded = jnp.concatenate([row_tokens, zero_rows], axis=1)
        dispatched = jax.vmap(lambda values, owners: values[owners // TOP])(padded, slot_owner)
        grouped = regroup(dispatched)
        pre_act = jnp.einsum("erd,def->erf", grouped.astype(jnp.float32), gate_float)
        gate_part = pre_act[..., :FF]
        up_part = pre_act[..., FF:]
        hidden = (jax.nn.silu(gate_part) * up_part).astype(jnp.bfloat16)
        outputs = jnp.einsum("erf,fed->erd", hidden.astype(jnp.float32), down_float).astype(jnp.bfloat16)
        picked = jax.vmap(lambda values, places: values[places])(ungroup(outputs), position)
        picked = picked.reshape(N_EXPERT, TOK_DEV, TOP, D).astype(jnp.float32)
        probs_float = row_probs.astype(jnp.float32)
        combined = jnp.sum(probs_float[..., None] * picked, axis=2).astype(jnp.bfloat16)
        cot_float = row_cot.astype(jnp.float32)
        prob_gradient = jnp.sum(cot_float[:, :, None, :] * picked, axis=3)
        scaled = (probs_float[..., None] * cot_float[:, :, None, :]).astype(jnp.bfloat16).reshape(N_EXPERT, TOK_DEV * TOP, D)
        scaled = jnp.concatenate([scaled, zero_rows], axis=1)
        cot_slots = regroup(jax.vmap(lambda values, owners: values[owners])(scaled, slot_owner))
        hidden_grad = jnp.einsum("erd,fed->erf", cot_slots.astype(jnp.float32), down_float)
        sigmoid_gate = jax.nn.sigmoid(gate_part)
        pre_gradient = jnp.concatenate([hidden_grad * up_part * sigmoid_gate * (1.0 + gate_part * (1.0 - sigmoid_gate)), hidden_grad * gate_part * sigmoid_gate], axis=-1).astype(jnp.bfloat16)
        input_grads = jnp.einsum("erf,def->erd", pre_gradient.astype(jnp.float32), gate_float).astype(jnp.bfloat16)
        returned = jax.vmap(lambda values, places: values[places])(ungroup(input_grads), position)
        token_gradient = jnp.sum(returned.reshape(N_EXPERT, TOK_DEV, TOP, D).astype(jnp.float32), axis=2).astype(jnp.bfloat16)
        grad_inner = jnp.einsum("erd,erf->def", grouped.astype(jnp.float32), pre_gradient.astype(jnp.float32))
        grad_down = jnp.einsum("erf,erd->fed", hidden.astype(jnp.float32), cot_slots.astype(jnp.float32))
        return (carry[0] + grad_inner, carry[1] + grad_down), (combined, token_gradient, prob_gradient)

    start_sums = (jnp.zeros((D, EXPERTS, 2 * FF), jnp.float32), jnp.zeros((FF, EXPERTS, D), jnp.float32))
    sums, row_outs = lax.scan(one_row, start_sums, (split_rows(tokens), split_rows(expert_ids), split_rows(gate_probs), split_rows(cotangent)))
    combined, token_gradient, prob_gradient = row_outs
    return join_rows(combined), join_rows(token_gradient), join_rows(prob_gradient), sums[0], sums[1]
```

```python
import jax
import jax.numpy as jnp
from jax import lax
from jax.sharding import PartitionSpec as P

CAP = 64
CORES = 2
BF = jnp.bfloat16
F32 = jnp.float32


def on_device(tokens, expert_ids, gate_probs, cotangent, gate_up, down_weights, *, sources, replicas):
    count, width = tokens.shape
    top = expert_ids.shape[1]
    local = gate_up.shape[1]
    hidden_width = down_weights.shape[0]
    cap = min(CAP, count)
    along = replicas // CORES
    replica = lax.axis_index("replica")
    core, place = lax.rem(replica, CORES), lax.div(replica, CORES)
    first = lax.axis_index("expert") * local
    slots = sources * cap

    all_ids = lax.all_gather(expert_ids.T, "expert", axis=0)
    all_probs = lax.all_gather(gate_probs.T, "expert", axis=0)
    all_tokens = lax.all_gather(tokens, "expert", axis=0, tiled=True)
    all_cot = lax.all_gather(cotangent, "expert", axis=0, tiled=True)

    named = (all_ids[None] == (first + jnp.arange(local, dtype=jnp.int32))[:, None, None, None])
    member = jnp.any(named, axis=2)
    weight = jnp.sum(jnp.where(named, all_probs[None].astype(F32), 0.0), axis=2)
    ahead = (jnp.arange(count)[:, None] < jnp.arange(count)[None, :]).astype(BF)
    rank = jnp.einsum("esp,pq->esq", member.astype(BF), ahead, preferred_element_type=F32)
    rank = jnp.where(member, rank.astype(jnp.int32), -1)
    chosen = rank[:, :, None, :] == jnp.arange(cap, dtype=jnp.int32)[None, None, :, None]
    same = jnp.arange(sources)[:, None] == jnp.arange(sources)[None, :]
    wide = chosen[:, :, :, None, :] & same[None, :, None, :, None]
    pick = wide.astype(BF).reshape(local * slots, sources * count)
    back = jnp.where(wide, weight[:, :, None, None, :], 0.0).astype(BF).reshape(local * slots, sources * count)
    slot_weight = jnp.sum(jnp.where(chosen, weight[:, :, None, :], 0.0), axis=3).reshape(local, slots, 1)

    def rows(values):
        return jnp.dot(pick, values, preferred_element_type=F32).astype(BF).reshape(local, slots, width)

    inputs = rows(all_tokens)
    raw_cot = rows(all_cot)
    out_grad = (slot_weight * raw_cot.astype(F32)).astype(BF)

    pair = [(i, i ^ 1) for i in range(replicas)]

    def swap(values):
        return lax.ppermute(values, "replica", pair)

    def columns(values, shift, side):
        size = values.shape[-1] // replicas
        block = lax.rem(place + shift, along) * CORES + side
        return lax.dynamic_slice_in_dim(values, block * size, size, 2)

    def shared_columns(values):
        theirs = swap(jnp.concatenate([columns(values, s, 1 - core) for s in range(along)], axis=2))
        size = values.shape[-1] // replicas
        return [
            jnp.concatenate([columns(values, s, core), theirs[:, :, s * size:(s + 1) * size]], axis=1)
            for s in range(along)
        ]

    def shared(values):
        return jnp.concatenate([values, swap(values)], axis=1)

    def summed(left, right):
        total = None
        for shift in list(range(1, along)) + [0]:
            part = jnp.einsum("era,erb->eab", left[shift], right, preferred_element_type=F32)
            if shift:
                step = [
                    (x * CORES + c, ((x + shift) % along) * CORES + c)
                    for x in range(along) for c in range(CORES)
                ]
                part = lax.ppermute(part.astype(BF), "replica", step).astype(F32)
            total = part if total is None else total + part
        return total.swapaxes(0, 1)

    input_columns = shared_columns(inputs)
    both_grad = shared(out_grad)

    pre_act = jnp.einsum("erd,def->erf", inputs, gate_up, preferred_element_type=F32)
    gate, up = pre_act[..., :hidden_width], pre_act[..., hidden_width:]
    sig = jax.nn.sigmoid(gate)
    hidden = (gate * sig * up).astype(BF)
    down_gradient = summed(shared_columns(hidden), both_grad)

    hidden_grad = jnp.einsum("erd,fed->erf", out_grad, down_weights, preferred_element_type=F32)
    pre_grad = jnp.concatenate(
        [hidden_grad * up * sig * (1.0 + gate * (1.0 - sig)), hidden_grad * gate * sig], axis=-1
    ).astype(BF)
    gate_up_gradient = summed(input_columns, shared(pre_grad))

    outputs = jnp.einsum("erf,fed->erd", hidden, down_weights, preferred_element_type=F32).astype(BF)
    input_grad = jnp.einsum("erf,def->erd", pre_grad, gate_up, preferred_element_type=F32).astype(BF)

    def returned(matrix, values):
        part = jnp.einsum(
            "ra,rd->ad", matrix, values.reshape(local * slots, width), preferred_element_type=F32
        ).astype(BF).reshape(sources, count, width)
        arrived = lax.all_to_all(part, "expert", split_axis=0, concat_axis=0, tiled=True)
        return jnp.sum(arrived.astype(F32), axis=0).astype(BF)

    combined = returned(back, outputs)
    token_gradient = returned(pick, input_grad)

    slot_prob = jnp.sum(raw_cot.astype(F32) * outputs.astype(F32), axis=2).reshape(local, sources, cap, 1)
    prob_part = jnp.sum(jnp.where(chosen, slot_prob, 0.0), axis=2).swapaxes(0, 1)
    prob_all = lax.all_to_all(prob_part, "expert", split_axis=0, concat_axis=0, tiled=True)
    prob_all = prob_all.reshape(sources * local, count)
    mine = expert_ids.T[:, None, :] == jnp.arange(sources * local, dtype=jnp.int32)[None, :, None]
    prob_gradient = jnp.sum(jnp.where(mine, prob_all[None], 0.0), axis=1).T
    return (combined, token_gradient, prob_gradient, gate_up_gradient, down_gradient)


def solution(mesh):
    rows = P(("groups", "expert", "replica"), None)
    sources, replicas = mesh.shape["expert"], mesh.shape["replica"]

    def body(*args):
        return on_device(*args, sources=sources, replicas=replicas)

    return jax.shard_map(
        body,
        mesh=mesh,
        in_specs=(rows, rows, rows, rows, P(None, "expert", None), P(None, "expert", None)),
        out_specs=(
            rows,
            rows,
            rows,
            P(("groups", "replica"), "expert", None),
            P(("groups", "replica"), "expert", None),
        ),
        check_vma=False,
    )
```

```python
import jax
import jax.numpy as jnp
from jax import lax
from jax.experimental.layout import Layout, with_layout_constraint
from jax.sharding import PartitionSpec as P


CAP = 64
CORES = 2
BF = jnp.bfloat16
F32 = jnp.float32


def on_device(tokens, expert_ids, gate_probs, cotangent, gate_up, down_weights, *, sources, replicas):
    count, width = tokens.shape
    top = expert_ids.shape[1]
    local = gate_up.shape[1]
    hidden_width = down_weights.shape[0]
    cap = min(CAP, count)
    along = replicas // CORES
    replica = lax.axis_index("replica")
    core, place = lax.rem(replica, CORES), lax.div(replica, CORES)
    first = lax.axis_index("expert") * local
    slots = sources * cap

    def to_source(values, shift):
        step = [(i, (i + shift) % sources) for i in range(sources)]
        return lax.ppermute(values, "expert", step) if shift else values

    notes = jnp.concatenate([expert_ids.T.astype(BF), gate_probs.T], axis=0)
    flat = notes.reshape(-1)
    extra = -(-flat.shape[0] // (16 * width)) * 16
    flat = jnp.pad(flat, (0, extra * width - flat.shape[0])).reshape(extra, width)
    packed = jnp.concatenate([tokens, flat], axis=0)
    held = [to_source(packed, s) for s in range(sources)]
    all_cot = jnp.concatenate([to_source(cotangent, s) for s in range(sources)], axis=0)
    all_tokens = jnp.concatenate([h[:count] for h in held], axis=0)
    all_notes = jnp.stack([h[count:].reshape(-1)[:notes.size].reshape(notes.shape) for h in held])
    all_ids = all_notes[:, :top].astype(jnp.int32)
    all_probs = all_notes[:, top:]

    named = (all_ids[None] == (first + jnp.arange(local, dtype=jnp.int32))[:, None, None, None])
    member = jnp.any(named, axis=2)
    weight = jnp.sum(jnp.where(named, all_probs[None].astype(F32), 0.0), axis=2)
    ahead = (jnp.arange(count)[:, None] < jnp.arange(count)[None, :]).astype(BF)
    rank = jnp.einsum("esp,pq->esq", member.astype(BF), ahead, preferred_element_type=F32)
    rank = jnp.where(member, rank.astype(jnp.int32), -1)
    chosen = rank[:, :, None, :] == jnp.arange(cap, dtype=jnp.int32)[None, None, :, None]
    same = jnp.arange(sources)[:, None] == jnp.arange(sources)[None, :]
    wide = chosen[:, :, :, None, :] & same[None, :, None, :, None]
    pick = wide.astype(BF).reshape(local * slots, sources * count)
    back = jnp.where(wide, weight[:, :, None, None, :], 0.0).astype(BF).reshape(local * slots, sources * count)
    slot_weight = jnp.sum(jnp.where(chosen, weight[:, :, None, :], 0.0), axis=3).reshape(local, slots, 1)

    def rows(values):
        return jnp.dot(pick, values, preferred_element_type=F32).astype(BF).reshape(local, slots, width)

    inputs = rows(all_tokens)
    raw_cot = rows(all_cot)
    out_grad = (slot_weight * raw_cot.astype(F32)).astype(BF)

    pair = [(i, i ^ 1) for i in range(replicas)]

    def swap(values):
        return lax.ppermute(values, "replica", pair)

    def columns(values, shift, side):
        size = values.shape[-1] // replicas
        block = lax.rem(place + shift, along) * CORES + side
        return lax.dynamic_slice_in_dim(values, block * size, size, 2)

    def shared_columns(values):
        theirs = swap(jnp.concatenate([columns(values, s, 1 - core) for s in range(along)], axis=2))
        size = values.shape[-1] // replicas
        return [
            jnp.concatenate([columns(values, s, core), theirs[:, :, s * size:(s + 1) * size]], axis=1)
            for s in range(along)
        ]

    def shared(values):
        return jnp.concatenate([values, swap(values)], axis=1)

    def part(left, right, shift):
        return jnp.einsum("era,erb->eab", left[shift], right, preferred_element_type=F32)

    def send_shares(left, right):
        shares = []
        for shift in range(1, along):
            share = part(left, right, shift).astype(BF).swapaxes(0, 1)
            share = with_layout_constraint(share, Layout((0, 1, 2)))
            shares.append(share)
        return shares

    def total(left, right, shares):
        own = with_layout_constraint(part(left, right, 0).swapaxes(0, 1), Layout((0, 1, 2)))
        for shift in range(1, along):
            step = [
                (x * CORES + c, ((x + shift) % along) * CORES + c)
                for x in range(along) for c in range(CORES)
            ]
            arrived = lax.ppermute(shares[shift - 1], "replica", step)
            own = own + arrived.astype(F32)
        return own

    input_columns = shared_columns(inputs)
    both_grad = shared(out_grad)

    pre_act = jnp.einsum("erd,def->erf", inputs, gate_up, preferred_element_type=F32)
    gate, up = pre_act[..., :hidden_width], pre_act[..., hidden_width:]
    sig = jax.nn.sigmoid(gate)
    hidden = (gate * sig * up).astype(BF)
    hidden_columns = shared_columns(hidden)
    outputs = jnp.einsum("erf,fed->erd", hidden, down_weights, preferred_element_type=F32).astype(BF)
    down_shares = send_shares(hidden_columns, both_grad)
    down_gradient = total(hidden_columns, both_grad, down_shares)
    if down_shares:
        later, _ = lax.optimization_barrier((out_grad, down_shares))
    else:
        later = out_grad

    hidden_grad = jnp.einsum("erd,fed->erf", later, down_weights, preferred_element_type=F32)
    pre_grad = jnp.concatenate(
        [hidden_grad * up * sig * (1.0 + gate * (1.0 - sig)), hidden_grad * gate * sig], axis=-1
    ).astype(BF)
    both_pre = shared(pre_grad)
    gate_shares = send_shares(input_columns, both_pre)
    gate_up_gradient = total(input_columns, both_pre, gate_shares)
    if gate_shares:
        after, _ = lax.optimization_barrier((pre_grad, gate_shares))
    else:
        after = pre_grad
    input_grad = jnp.einsum("erf,def->erd", after, gate_up, preferred_element_type=F32).astype(BF)

    def returned(matrix, values):
        parts = jnp.einsum(
            "ra,rd->ad", matrix, values.reshape(local * slots, width), preferred_element_type=F32
        ).astype(BF).reshape(sources, count, width)
        arrived = [to_source(parts[s], -s).astype(F32) for s in range(sources)]
        return sum(arrived[1:], arrived[0]).astype(BF)

    combined = returned(back, outputs)
    token_gradient = returned(pick, input_grad)

    slot_prob = jnp.sum(raw_cot.astype(F32) * outputs.astype(F32), axis=2).reshape(local, sources, cap, 1)
    prob_part = jnp.sum(jnp.where(chosen, slot_prob, 0.0), axis=2).swapaxes(0, 1)
    choice = expert_ids.T
    prob_gradient = jnp.zeros((top, count), F32)
    home = lax.axis_index("expert")
    for s in range(sources):
        block = lax.rem(home + s, sources) * local
        theirs = to_source(prob_part[s], -s)
        hit = choice[:, None, :] == (block + jnp.arange(local, dtype=jnp.int32))[None, :, None]
        prob_gradient = prob_gradient + jnp.sum(jnp.where(hit, theirs[None], 0.0), axis=1)
    prob_gradient = prob_gradient.T
    return (combined, token_gradient, prob_gradient, gate_up_gradient, down_gradient)


def solution(mesh):
    rows = P(("groups", "expert", "replica"), None)
    sources, replicas = mesh.shape["expert"], mesh.shape["replica"]

    def body(*args):
        return on_device(*args, sources=sources, replicas=replicas)

    return jax.shard_map(
        body,
        mesh=mesh,
        in_specs=(rows, rows, rows, rows, P(None, "expert", None), P(None, "expert", None)),
        out_specs=(
            rows,
            rows,
            rows,
            P(("groups", "replica"), "expert", None),
            P(("groups", "replica"), "expert", None),
        ),
        check_vma=False,
    )
```

```python
import jax
import jax.numpy as jnp
from jax import lax
from jax.experimental.layout import Layout, with_layout_constraint
from jax.sharding import PartitionSpec as P


CAP = 64
CORES = 2
BF = jnp.bfloat16
F32 = jnp.float32


def on_device(tokens, expert_ids, gate_probs, cotangent, gate_up, down_weights, *, sources, replicas):
    count, width = tokens.shape
    top = expert_ids.shape[1]
    local = gate_up.shape[1]
    hidden_width = down_weights.shape[0]
    cap = min(CAP, count)
    along = replicas // CORES
    replica = lax.axis_index("replica")
    core, place = lax.rem(replica, CORES), lax.div(replica, CORES)
    first = lax.axis_index("expert") * local
    slots = sources * cap

    def to_source(values, shift):
        step = [(i, (i + shift) % sources) for i in range(sources)]
        return lax.ppermute(values, "expert", step) if shift else values

    notes = jnp.concatenate([expert_ids.T.astype(BF), gate_probs.T], axis=0)
    flat = notes.reshape(-1)
    extra = -(-flat.shape[0] // (16 * width)) * 16
    flat = jnp.pad(flat, (0, extra * width - flat.shape[0])).reshape(extra, width)
    packed = jnp.concatenate([tokens, flat], axis=0)
    held = [to_source(packed, s) for s in range(sources)]
    all_cot = jnp.concatenate([to_source(cotangent, s) for s in range(sources)], axis=0)
    all_tokens = jnp.concatenate([h[:count] for h in held], axis=0)
    all_notes = jnp.stack([h[count:].reshape(-1)[:notes.size].reshape(notes.shape) for h in held])
    all_ids = all_notes[:, :top].astype(jnp.int32)
    all_probs = all_notes[:, top:]

    named = (all_ids[None] == (first + jnp.arange(local, dtype=jnp.int32))[:, None, None, None])
    member = jnp.any(named, axis=2)
    weight = jnp.sum(jnp.where(named, all_probs[None].astype(F32), 0.0), axis=2)
    ahead = (jnp.arange(count)[:, None] < jnp.arange(count)[None, :]).astype(BF)
    rank = jnp.einsum("esp,pq->esq", member.astype(BF), ahead, preferred_element_type=F32)
    rank = jnp.where(member, rank.astype(jnp.int32), -1)
    chosen = rank[:, :, None, :] == jnp.arange(cap, dtype=jnp.int32)[None, None, :, None]
    same = jnp.arange(sources)[:, None] == jnp.arange(sources)[None, :]
    wide = chosen[:, :, :, None, :] & same[None, :, None, :, None]
    pick = wide.astype(BF).reshape(local * slots, sources * count)
    back = jnp.where(wide, weight[:, :, None, None, :], 0.0).astype(BF).reshape(local * slots, sources * count)
    slot_weight = jnp.sum(jnp.where(chosen, weight[:, :, None, :], 0.0), axis=3).reshape(local, slots, 1)

    def rows(values):
        return jnp.dot(pick, values, preferred_element_type=F32).astype(BF).reshape(local, slots, width)

    inputs = rows(all_tokens)

    pair = [(i, i ^ 1) for i in range(replicas)]

    def swap(values):
        return lax.ppermute(values, "replica", pair)

    def columns(values, shift, side):
        size = values.shape[-1] // replicas
        block = lax.rem(place + shift, along) * CORES + side
        return lax.dynamic_slice_in_dim(values, block * size, size, 2)

    def sent_columns(values):
        return jnp.concatenate([columns(values, s, 1 - core) for s in range(along)], axis=2)

    def shared_columns(values, sent):
        theirs = swap(sent)
        size = values.shape[-1] // replicas
        return [
            jnp.concatenate([columns(values, s, core), theirs[:, :, s * size:(s + 1) * size]], axis=1)
            for s in range(along)
        ]

    def shared(values):
        return jnp.concatenate([values, swap(values)], axis=1)

    def part(left, right, shift):
        return jnp.einsum("era,erb->eab", left[shift], right, preferred_element_type=F32)

    def send_shares(left, right):
        shares = []
        for shift in range(1, along):
            share = part(left, right, shift).astype(BF).swapaxes(0, 1)
            share = with_layout_constraint(share, Layout((0, 1, 2)))
            shares.append(share)
        return shares

    def arrivals(shares):
        added = jnp.zeros((), F32)
        for shift in range(1, along):
            step = [
                (x * CORES + c, ((x + shift) % along) * CORES + c)
                for x in range(along) for c in range(CORES)
            ]
            arrived = lax.ppermute(shares[shift - 1], "replica", step)
            added = added + arrived.astype(F32)
        return added

    def total(left, right, shares):
        own = with_layout_constraint(part(left, right, 0).swapaxes(0, 1), Layout((0, 1, 2)))
        return own + arrivals(shares)

    pre_act = jnp.einsum("erd,def->erf", inputs, gate_up, preferred_element_type=F32)
    gate, up = pre_act[..., :hidden_width], pre_act[..., hidden_width:]
    sig = jax.nn.sigmoid(gate)
    hidden = (gate * sig * up).astype(BF)
    outputs = jnp.einsum("erf,fed->erd", hidden, down_weights, preferred_element_type=F32).astype(BF)
    input_sent, hidden_sent = sent_columns(inputs), sent_columns(hidden)
    all_cot, input_sent, hidden_sent, outputs = lax.optimization_barrier(
        (all_cot, input_sent, hidden_sent, outputs)
    )
    input_columns = shared_columns(inputs, input_sent)
    hidden_columns = shared_columns(hidden, hidden_sent)

    raw_cot = rows(all_cot)
    out_grad = (slot_weight * raw_cot.astype(F32)).astype(BF)
    both_grad = shared(out_grad)

    down_shares = send_shares(hidden_columns, both_grad)
    down_gradient = total(hidden_columns, both_grad, down_shares)
    if down_shares:
        later, _ = lax.optimization_barrier((out_grad, down_shares))
    else:
        later = out_grad

    hidden_grad = jnp.einsum("erd,fed->erf", later, down_weights, preferred_element_type=F32)
    pre_grad = jnp.concatenate(
        [hidden_grad * up * sig * (1.0 + gate * (1.0 - sig)), hidden_grad * gate * sig], axis=-1
    ).astype(BF)
    both_pre = shared(pre_grad)
    rows_out = width // replicas
    cuts = 2 if rows_out % 256 == 0 else 1
    pieces = [
        [c[:, :, i * rows_out // cuts:(i + 1) * rows_out // cuts] for c in input_columns]
        for i in range(cuts)
    ]
    gate_shares = [send_shares(piece, both_pre) for piece in pieces]
    gate_up_gradient = lax.optimization_barrier(
        with_layout_constraint(part(input_columns, both_pre, 0).swapaxes(0, 1), Layout((0, 1, 2)))
    )
    for i in range(cuts):
        at = i * rows_out // cuts
        added = gate_up_gradient[at:at + rows_out // cuts] + arrivals(gate_shares[i])
        gate_up_gradient = lax.dynamic_update_slice_in_dim(gate_up_gradient, added, at, 0)
    if gate_shares[0]:
        after, _ = lax.optimization_barrier((pre_grad, gate_shares))
    else:
        after = pre_grad
    input_grad = jnp.einsum("erf,def->erd", after, gate_up, preferred_element_type=F32).astype(BF)

    def returned(matrix, values):
        parts = jnp.einsum(
            "ra,rd->ad", matrix, values.reshape(local * slots, width), preferred_element_type=F32
        ).astype(BF).reshape(sources, count, width)
        arrived = [to_source(parts[s], -s).astype(F32) for s in range(sources)]
        return sum(arrived[1:], arrived[0]).astype(BF)

    combined = returned(back, outputs)
    token_gradient = returned(pick, input_grad)

    slot_prob = jnp.sum(raw_cot.astype(F32) * outputs.astype(F32), axis=2).reshape(local, sources, cap, 1)
    prob_part = jnp.sum(jnp.where(chosen, slot_prob, 0.0), axis=2).swapaxes(0, 1)
    choice = expert_ids.T
    prob_gradient = jnp.zeros((top, count), F32)
    home = lax.axis_index("expert")
    for s in range(sources):
        block = lax.rem(home + s, sources) * local
        theirs = to_source(prob_part[s], -s)
        hit = choice[:, None, :] == (block + jnp.arange(local, dtype=jnp.int32))[None, :, None]
        prob_gradient = prob_gradient + jnp.sum(jnp.where(hit, theirs[None], 0.0), axis=1)
    prob_gradient = prob_gradient.T
    return (combined, token_gradient, prob_gradient, gate_up_gradient, down_gradient)


def solution(mesh):
    rows = P(("groups", "expert", "replica"), None)
    sources, replicas = mesh.shape["expert"], mesh.shape["replica"]

    def body(*args):
        return on_device(*args, sources=sources, replicas=replicas)

    return jax.shard_map(
        body,
        mesh=mesh,
        in_specs=(rows, rows, rows, rows, P(None, "expert", None), P(None, "expert", None)),
        out_specs=(
            rows,
            rows,
            rows,
            P(("groups", "replica"), "expert", None),
            P(("groups", "replica"), "expert", None),
        ),
        check_vma=False,
    )
```
